32 devices in a mesh: dp: 16 (over z, x, core), tensor: 2 (over y).
Axes of the slice: x: 2, y: 2, z: 4, core: 2. Of those that a mesh axis runs over, the one named last changes fastest.
Arguments:
- text_states: bfloat16 [23552, 768], P(('dp', 'tensor')), may hold values from -6 to 6
- image_states: bfloat16 [9216, 1024], P(('dp', 'tensor')), may hold values from -6 to 6
- caption_lengths: int32 [256], P('dp'), may hold values from 2 to 92, as said below
- text_grad: bfloat16 [23552, 768], P(('dp', 'tensor')), may hold values from -18 to 18
- image_grad: bfloat16 [9216, 1024], P(('dp', 'tensor')), may hold values from -18 to 18
- text_query: bfloat16 [768, 1024], P(None, 'tensor'), may hold values from -0.21875 to 0.21875
- text_keyval: bfloat16 [768, 2, 1024], P(None, None, 'tensor'), may hold values from -0.21875 to 0.21875
- text_output: bfloat16 [1024, 768], P('tensor'), may hold values from -1 to 1
- text_up: bfloat16 [768, 3072], P(None, 'tensor'), may hold values from -0.21875 to 0.21875
- text_up_bias: bfloat16 [3072], P('tensor'), may hold values from -3 to 3
- text_down: bfloat16 [3072, 768], P('tensor'), may hold values from -0.109375 to 0.109375
- text_gains: bfloat16 [2, 768], replicated, may hold values from 0.5 to 1.5
- text_shifts: bfloat16 [4, 768], replicated, may hold values from -3 to 3
- image_query: bfloat16 [1024, 1024], P(None, 'tensor'), may hold values from -0.1875 to 0.1875
- image_keyval: bfloat16 [1024, 2, 1024], P(None, None, 'tensor'), may hold values from -0.1875 to 0.1875
- image_output: bfloat16 [1024, 1024], P('tensor'), may hold values from -1 to 1
- image_up: bfloat16 [1024, 1024], P(None, 'tensor'), may hold values from -0.1875 to 0.1875
- image_up_bias: bfloat16 [1024], P('tensor'), may hold values from -3 to 3
- image_down: bfloat16 [1024, 1024], P('tensor'), may hold values from -0.1875 to 0.1875
- image_gains: bfloat16 [2, 1024], replicated, may hold values from 0.5 to 1.5
- image_shifts: bfloat16 [4, 1024], replicated, may hold values from -3 to 3
Outputs:
- text_out: bfloat16 [23552, 768], P(('dp', 'tensor'))
- image_out: bfloat16 [9216, 1024], P(('dp', 'tensor'))
- text_input_grad: bfloat16 [23552, 768], P(('dp', 'tensor'))
- image_input_grad: bfloat16 [9216, 1024], P(('dp', 'tensor'))
- text_query_grad: float32 [768, 1024], P(None, 'tensor')
- text_keyval_grad: float32 [768, 2, 1024], P(None, None, 'tensor')
- text_output_grad: float32 [1024, 768], P('tensor')
- text_up_grad: float32 [768, 3072], P(None, 'tensor')
- text_up_bias_grad: float32 [3072], P('tensor')
- text_down_grad: float32 [3072, 768], P('tensor')
- text_gains_grad: float32 [2, 768], replicated
- text_shifts_grad: float32 [4, 768], replicated
- image_query_grad: float32 [1024, 1024], P(None, 'tensor')
- image_keyval_grad: float32 [1024, 2, 1024], P(None, None, 'tensor')
- image_output_grad: float32 [1024, 1024], P('tensor')
- image_up_grad: float32 [1024, 1024], P(None, 'tensor')
- image_up_bias_grad: float32 [1024], P('tensor')
- image_down_grad: float32 [1024, 1024], P('tensor')
- image_gains_grad: float32 [2, 1024], replicated
- image_shifts_grad: float32 [4, 1024], replicated
The draws below stay inside these ranges and needn't reach their ends.
Inputs may be any that keep to these rules, and one draw needn't show every extreme that they name: caption_lengths: the caption tokens of each pair that are real; positions from it to 91 are padding. Some pair has all 92 and some pair only 2.
All inputs are finite; a program needn't handle non-finite values.
Results may differ from the reference program's by a relative error of at most 0.015.
Values may be sent and summed in bfloat16 or wider, within the bound.
No kernel may reach another device: no remote copies, remote signals or barrier semaphores. Data moves between devices by JAX's collectives and lax.ppermute only.
A program may use at most 192 MiB of HBM per device.

```python
import jax
import jax.numpy as jnp
from jax import lax

DT = 768
DV = 1024
INNER = 1024
FT = 3072
FV = 1024
CAP = 92
REGIONS = 36
PAIRS_DEV = 16
HDIM = 128
PAIRS = 256
TEXT = 23552
IMAGE = 9216


def draw_caption_lengths(key, part):
    draw_key, place_key = jax.random.split(jax.random.fold_in(key, 11))
    lengths = jax.random.randint(draw_key, (PAIRS,), 2, CAP + 1, dtype=jnp.int32)
    places = jax.random.permutation(place_key, PAIRS)
    return lengths.at[places[0]].set(CAP).at[places[1]].set(2)


def rising_rows(key, row_count, columns):
    row_scale = 1.0 + 2.0 * jnp.arange(row_count, dtype=jnp.float32)[:, None] / max(row_count - 1, 1)
    sample = jnp.clip(jax.random.normal(key, (row_count, columns), jnp.float32), -6.0, 6.0)
    return sample * row_scale


def draw_text_grad(key, part):
    return rising_rows(jax.random.fold_in(key, 21), TEXT, DT).astype(jnp.bfloat16)


def draw_image_grad(key, part):
    return rising_rows(jax.random.fold_in(key, 31), IMAGE, DV).astype(jnp.bfloat16)


def shard_levels(key, extent, shards, smallest, largest):
    factor_of, own = 1.0, jax.random.fold_in(key, 6)
    for axis_at, shards_of in shards:
        steps = jnp.exp(jax.random.uniform(jax.random.fold_in(own, axis_at), (shards_of,), jnp.float32, smallest / len(shards), largest / len(shards)))
        factor_of = factor_of * jnp.repeat(steps, extent[axis_at] // shards_of).reshape([-1 if axis == axis_at else 1 for axis in range(len(extent))])
    return factor_of


def centred(rng, extent, spread, limit, cuts=(), kind=jnp.bfloat16):
    loudness = shard_levels(rng, extent, cuts, -0.22, 0.18) if cuts else 1.0
    values = jax.random.normal(rng, extent, jnp.float32) * spread * loudness
    return jnp.minimum(jnp.maximum(values, -limit), limit).astype(kind)


def setup_inputs(seed: int = 0) -> dict:
    key_of = jax.random.split(jax.random.key(seed), 22)
    return {
        "text_states": centred(key_of[0], (TEXT, DT), 1.0, 6.0, ((0, 32),)),
        "image_states": centred(key_of[1], (IMAGE, DV), 1.0, 6.0, ((0, 32),)),
        "caption_lengths": draw_caption_lengths(jax.random.fold_in(key_of[21], 71), 0),
        "text_grad": draw_text_grad(jax.random.fold_in(key_of[21], 71), 0),
        "image_grad": draw_image_grad(jax.random.fold_in(key_of[21], 71), 0),
        "text_query": centred(key_of[5], (DT, INNER), DT ** -0.5, 0.21875, ((1, 2),)),
        "text_keyval": centred(key_of[6], (DT, 2, INNER), DT ** -0.5, 0.21875, ((2, 2),)),
        "text_output": centred(key_of[7], (INNER, DT), (INNER // 32) ** -0.5, 1.0, ((0, 2),)),
        "text_up": centred(key_of[8], (DT, FT), DT ** -0.5, 0.21875, ((1, 2),)),
        "text_up_bias": centred(key_of[9], (FT,), 0.5, 3.0, ((0, 2),)),
        "text_down": centred(key_of[10], (FT, DT), FT ** -0.5, 0.109375, ((0, 2),)),
        "text_gains": jnp.clip(1.0 + 0.1 * jax.random.normal(key_of[11], (2, DT), jnp.float32), 0.5, 1.5).astype(jnp.bfloat16),
        "text_shifts": centred(key_of[12], (4, DT), 0.5, 3.0),
        "image_query": centred(key_of[13], (DV, INNER), DV ** -0.5, 0.1875, ((1, 2),)),
        "image_keyval": centred(key_of[14], (DV, 2, INNER), DV ** -0.5, 0.1875, ((2, 2),)),
        "image_output": centred(key_of[15], (INNER, DV), (INNER // 32) ** -0.5, 1.0, ((0, 2),)),
        "image_up": centred(key_of[16], (DV, FV), DV ** -0.5, 0.1875, ((1, 2),)),
        "image_up_bias": centred(key_of[17], (FV,), 0.5, 3.0, ((0, 2),)),
        "image_down": centred(key_of[18], (FV, DV), FV ** -0.5, 0.1875, ((0, 2),)),
        "image_gains": jnp.clip(1.0 + 0.1 * jax.random.normal(key_of[19], (2, DV), jnp.float32), 0.5, 1.5).astype(jnp.bfloat16),
        "image_shifts": centred(key_of[20], (4, DV), 0.5, 3.0),
    }


@jax.custom_vjp
def low(v):
    return lax.optimization_barrier(v.astype(jnp.bfloat16)).astype(jnp.float32)

@jax.custom_vjp
def low_back(v):
    return v

def low_keep(v):
    return (low(v), None)

def low_pass(kept, grad):
    return (grad,)

def back_keep(v):
    return (v, None)

def back_low(kept, grad):
    return (low(grad),)
low.defvjp(low_keep, low_pass)
low_back.defvjp(back_keep, back_low)

def matmul(left, right):
    return jnp.dot(left, right, precision=lax.Precision.HIGHEST)

def layer_norm(hidden, gain, shift):
    centre = hidden - lax.optimization_barrier(jnp.mean(hidden, axis=-1, keepdims=True))
    scaled = centre * lax.rsqrt(lax.optimization_barrier(jnp.mean(centre * centre, axis=-1, keepdims=True)) + 1e-06)
    return scaled * gain + shift

def split_heads(rows, length):
    return rows.reshape(rows.shape[0] // length, length, rows.shape[1] // HDIM, HDIM)

def attend(queries, key_vals, length_q, length_k, key_valid):
    query_heads = split_heads(queries, length_q)
    key_heads = split_heads(key_vals[:, 0], length_k)
    value_heads = split_heads(key_vals[:, 1], length_k)
    scores = jnp.einsum('gqhd,gkhd->ghqk', query_heads, key_heads, precision=lax.Precision.HIGHEST) * HDIM ** (-0.5)
    scores = low_back(scores)
    if key_valid is not None:
        scores = jnp.where(key_valid, scores, -1e+30)
    weights = low(jax.nn.softmax(scores, axis=-1))
    context = jnp.einsum('ghqk,gkhd->gqhd', weights, value_heads, precision=lax.Precision.HIGHEST)
    return low(low_back(context.reshape(queries.shape)))

def finish(states, context, output_w, up_w, up_bias, down_w, gains, shifts):
    branch = low_back(matmul(context, output_w) + shifts[0])
    normed = layer_norm(states + branch, gains[0], shifts[1])
    hidden = low_back(matmul(low(normed), up_w) + up_bias)
    active = low(jax.nn.gelu(hidden, approximate=False))
    result = low_back(matmul(active, down_w) + shifts[2])
    return layer_norm(normed + result, gains[1], shifts[3])

def project(states, query_w, keyval_w):
    queries = low(low_back(matmul(states, query_w)))
    key_vals = low(low_back(jnp.einsum('nd,dki->nki', states, keyval_w, precision=lax.Precision.HIGHEST)))
    return (queries, key_vals)

def forward(params, text_states, image_states, lengths):
    text_q, text_kv = project(low(text_states), params[0], params[1])
    image_q, image_kv = project(low(image_states), params[8], params[9])
    key_valid = (jnp.arange(CAP)[None, :] < lengths[:, None])[:, None, None, :]
    text_ctx = attend(text_q, image_kv, CAP, REGIONS, None)
    image_ctx = attend(image_q, text_kv, REGIONS, CAP, key_valid)
    text_final = finish(text_states, text_ctx, params[2], params[3], params[4], params[5], params[6], params[7])
    image_final = finish(image_states, image_ctx, params[10], params[11], params[12], params[13], params[14], params[15])
    return (text_final, image_final)

def add_trees(left_tree, right_tree):
    return jax.tree.map(lambda left_leaf, right_leaf: left_leaf + right_leaf, left_tree, right_tree)

def reference(text_states, image_states, caption_lengths, text_grad, image_grad, text_query, text_keyval, text_output, text_up, text_up_bias, text_down, text_gains, text_shifts, image_query, image_keyval, image_output, image_up, image_up_bias, image_down, image_gains, image_shifts):
    raw_params = (text_query, text_keyval, text_output, text_up, text_up_bias, text_down, text_gains, text_shifts, image_query, image_keyval, image_output, image_up, image_up_bias, image_down, image_gains, image_shifts)
    params = tuple((member.astype(jnp.float32) for member in raw_params))
    blocks = PAIRS // PAIRS_DEV
    text_blocks = text_states.astype(jnp.float32).reshape(blocks, PAIRS_DEV * CAP, DT)
    image_blocks = image_states.astype(jnp.float32).reshape(blocks, PAIRS_DEV * REGIONS, DV)
    text_cots = text_grad.astype(jnp.float32).reshape(blocks, PAIRS_DEV * CAP, DT)
    image_cots = image_grad.astype(jnp.float32).reshape(blocks, PAIRS_DEV * REGIONS, DV)
    length_blocks = caption_lengths.reshape(blocks, PAIRS_DEV)

    def one_block(totals, inputs):
        text_rows, image_rows, lengths, text_cot, image_cot = inputs

        def block_forward(block_params, text_part, image_part):
            return forward(block_params, text_part, image_part, lengths)
        outputs, pullback = jax.vjp(block_forward, params, text_rows, image_rows)
        param_grads, text_dx, image_dx = pullback((text_cot, image_cot))
        return (add_trees(totals, param_grads), (outputs[0], outputs[1], text_dx, image_dx))
    zero_grads = jax.tree.map(jnp.zeros_like, params)
    totals, stacked = lax.scan(one_block, zero_grads, (text_blocks, image_blocks, length_blocks, text_cots, image_cots))
    text_out = stacked[0].reshape(TEXT, DT).astype(jnp.bfloat16)
    image_out = stacked[1].reshape(IMAGE, DV).astype(jnp.bfloat16)
    text_dx = stacked[2].reshape(TEXT, DT).astype(jnp.bfloat16)
    image_dx = stacked[3].reshape(IMAGE, DV).astype(jnp.bfloat16)
    return (text_out, image_out, text_dx, image_dx, totals[0], totals[1], totals[2], totals[3], totals[4], totals[5], totals[6], totals[7], totals[8], totals[9], totals[10], totals[11], totals[12], totals[13], totals[14], totals[15])
```

```python
import functools

import jax
import jax.numpy as jnp
from jax import lax
from jax.experimental import pallas as pl
from jax.experimental.pallas import tpu as pltpu
from jax.sharding import PartitionSpec as P

CAP = 92
REGIONS = 36
HDIM = 128
GROUP = 4
SCALE = HDIM ** (-0.5)
NEG = -1e30
BF = jnp.bfloat16
F32 = jnp.float32


def dot(a, b):
    return jnp.dot(a, b, preferred_element_type=F32)


def dot_nt(a, b):
    return lax.dot_general(a, b, (((1,), (1,)), ((), ())), preferred_element_type=F32)


def dot_tn(a, b):
    return lax.dot_general(a, b, (((0,), (0,)), ((), ())), preferred_element_type=F32)


def pair_ids(rows, length, axis, shape):
    at = lax.broadcasted_iota(jnp.int32, shape, axis)
    ids = jnp.zeros(shape, jnp.int32)
    for k in range(1, rows // length):
        ids = ids + (at >= k * length).astype(jnp.int32)
    return at, ids


def block_masks(lens_ref, text_rows, image_rows):
    first = pl.program_id(0) * GROUP
    _, text_row = pair_ids(text_rows, CAP, 0, (text_rows, 1))
    _, image_col = pair_ids(image_rows, REGIONS, 1, (1, image_rows))
    text_mask = text_row == image_col
    _, image_row = pair_ids(image_rows, REGIONS, 0, (image_rows, 1))
    at, text_col = pair_ids(text_rows, CAP, 1, (1, text_rows))
    for k in range(GROUP):
        stop = k * CAP + lens_ref[first + k]
        text_col = jnp.where((text_col == k) & (at >= stop), -1, text_col)
    image_mask = image_row == text_col
    return text_mask, image_mask


def softmax(scores, mask):
    scores = jnp.where(mask, scores * SCALE, NEG)
    top = jnp.max(scores, axis=-1, keepdims=True)
    exponent = jnp.exp(scores - top)
    return exponent / jnp.sum(exponent, axis=-1, keepdims=True)


def attend_kernel(lens_ref, text_ref, image_ref, text_ctx_ref, image_ctx_ref):
    width = text_ctx_ref.shape[1]
    masks = block_masks(lens_ref, text_ref.shape[0], image_ref.shape[0])
    for at in range(0, width, HDIM):
        for mask, mine, other, out in (
            (masks[0], text_ref, image_ref, text_ctx_ref),
            (masks[1], image_ref, text_ref, image_ctx_ref),
        ):
            query = mine[:, at : at + HDIM]
            key = other[:, width + at : width + at + HDIM]
            value = other[:, 2 * width + at : 2 * width + at + HDIM]
            probs = softmax(dot_nt(query, key), mask)
            out[:, at : at + HDIM] = dot(probs.astype(BF), value).astype(BF)


def attend_back_kernel(lens_ref, text_ref, image_ref, text_dc_ref, image_dc_ref, dtext_ref, dimage_ref):
    width = text_dc_ref.shape[1]
    masks = block_masks(lens_ref, text_ref.shape[0], image_ref.shape[0])
    for at in range(0, width, HDIM):
        for mask, mine, other, grad, dmine, dother in (
            (masks[0], text_ref, image_ref, text_dc_ref, dtext_ref, dimage_ref),
            (masks[1], image_ref, text_ref, image_dc_ref, dimage_ref, dtext_ref),
        ):
            q_at, k_at, v_at = (slice(at + i * width, at + i * width + HDIM) for i in range(3))
            query, key, value = mine[:, q_at], other[:, k_at], other[:, v_at]
            dctx = grad[:, q_at]
            probs = softmax(dot_nt(query, key), mask)
            dprobs = dot_nt(dctx, value)
            delta = jnp.sum(probs * dprobs, axis=-1, keepdims=True)
            dscores = (probs * (dprobs - delta)).astype(BF)
            dmine[:, q_at] = (dot(dscores, key) * SCALE).astype(BF)
            dother[:, k_at] = (dot_tn(dscores, query) * SCALE).astype(BF)
            dother[:, v_at] = dot_tn(probs.astype(BF), dctx).astype(BF)


def attend_call(kernel, lens, arrays, out_widths, name):
    pairs = lens.shape[0]
    steps = pairs // GROUP
    rows = (GROUP * CAP, GROUP * REGIONS)

    def spec(stream, width):
        return pl.BlockSpec((rows[stream], width), lambda i, lens_ref: (i, 0))

    in_specs = [spec(i % 2, a.shape[1]) for i, a in enumerate(arrays)]
    outs = [
        jax.ShapeDtypeStruct((rows[i] * steps, width), BF) for i, width in enumerate(out_widths)
    ]
    return pl.pallas_call(
        kernel,
        grid_spec=pltpu.PrefetchScalarGridSpec(
            num_scalar_prefetch=1,
            grid=(steps,),
            in_specs=in_specs,
            out_specs=[spec(i, width) for i, width in enumerate(out_widths)],
        ),
        out_shape=outs,
        name=name,
    )(lens, *arrays)


def layer_norm(hidden, gain, shift):
    centre = hidden - jnp.mean(hidden, axis=-1, keepdims=True)
    inv_std = lax.rsqrt(jnp.mean(centre * centre, axis=-1, keepdims=True) + 1e-06)
    scaled = centre * inv_std
    return (scaled * gain + shift, scaled, inv_std)


def norm_backward(grad_out, scaled, inv_std, gain):
    grad_scaled = grad_out * gain
    mean_grad = jnp.mean(grad_scaled, axis=-1, keepdims=True)
    mean_dot = jnp.mean(grad_scaled * scaled, axis=-1, keepdims=True)
    return inv_std * (grad_scaled - mean_grad - scaled * mean_dot)


def column_sum(values):
    return jnp.sum(values.astype(F32), axis=0)


def half(array, bit):
    size = array.shape[0] // 2
    return lax.dynamic_slice_in_dim(array, bit * size, size, 0)


def join(mine, other, bit):
    return jnp.where(
        bit == 0, jnp.concatenate([mine, other], 0), jnp.concatenate([other, mine], 0)
    )


class Links:
    def __init__(self, dp_size):
        self.size = dp_size
        self.at = lax.axis_index("dp")
        self.masks = []
        mask = 1
        while mask < dp_size:
            self.masks.append(mask)
            mask *= 2

    def bit(self, mask):
        return (self.at // mask) % 2

    def swap(self, array, mask):
        return lax.ppermute(array, "dp", [(i, i ^ mask) for i in range(self.size)])

    def across(self, array):
        return lax.ppermute(array, "tensor", [(0, 1), (1, 0)])

    def fetch(self, own):
        core, near = self.bit(1), self.bit(2)
        piece = self.across(half(half(own, core), near))
        part = join(piece, self.swap(piece, 2), near)
        return join(part, self.swap(part, 1), core)

    def reduce(self, own, other):
        core = self.bit(1)
        kept = half(other, core) + self.swap(half(other, 1 - core), 1)
        mine = half(own, core).astype(F32) + self.swap(half(own, 1 - core), 1).astype(F32)
        total = (mine + self.across(kept).astype(F32)).astype(BF)
        for mask in self.masks[1:]:
            bit = self.bit(mask)
            total = half(total, bit) + self.swap(half(total, 1 - bit), mask)
        for mask in self.masks[:0:-1]:
            total = join(total, self.swap(total, mask), self.bit(mask))
        return join(total, self.swap(total, 1), core).astype(F32)

    def reduce_small(self, values):
        values = values + lax.ppermute(values, "tensor", [(0, 1), (1, 0)])
        for mask in self.masks:
            values = values + self.swap(values, mask)
        return values


def stream_middle(states, branch, gain, shift, grad, ups, biases, downs):
    normed, scaled1, inv1 = layer_norm(states.astype(F32) + (branch + shift[0]), gain[0], shift[1])
    rows = normed.astype(BF)
    actives, slopes = [], []
    result = None
    for up, bias, down in zip(ups, biases, downs):
        hidden = dot(rows, up) + bias.astype(F32)
        phi = 0.5 * (1.0 + lax.erf(hidden * 0.7071067811865476))
        active = (hidden * phi).astype(BF)
        actives.append(active)
        slopes.append(phi + hidden * jnp.exp(-0.5 * hidden * hidden) * 0.3989422804014327)
        term = dot(active, down)
        result = term if result is None else result + term
    final, scaled2, inv2 = layer_norm(normed + (result + shift[2]), gain[1], shift[3])
    out = final.astype(BF)
    cot = grad.astype(F32)
    gain2 = jnp.sum(cot * scaled2, axis=0)
    shift3 = jnp.sum(cot, axis=0)
    dh2 = norm_backward(cot, scaled2, inv2, gain[1])
    dy2 = dh2.astype(BF)
    shift2 = column_sum(dy2)
    down_grads, up_grads, bias_grads = [], [], []
    dn1 = dh2
    for up, down, active, slope in zip(ups, downs, actives, slopes):
        down_grads.append(dot_tn(active, dy2).astype(BF))
        dhidden = (dot_nt(dy2, down) * slope).astype(BF)
        bias_grads.append(column_sum(dhidden))
        up_grads.append(dot_tn(rows, dhidden).astype(BF))
        dn1 = dn1 + dot_nt(dhidden, up)
    gain1 = jnp.sum(dn1 * scaled1, axis=0)
    shift1 = jnp.sum(dn1, axis=0)
    dh1 = norm_backward(dn1, scaled1, inv1, gain[0])
    dout = dh1.astype(BF)
    shift0 = column_sum(dout)
    small = jnp.concatenate([gain1, gain2, shift0, shift1, shift2, shift3])
    return out, dh1, dout, down_grads, up_grads, bias_grads, small


def per_device(
    dp_size,
    text_states,
    image_states,
    caption_lengths,
    text_grad,
    image_grad,
    text_query,
    text_keyval,
    text_output,
    text_up,
    text_up_bias,
    text_down,
    text_gains,
    text_shifts,
    image_query,
    image_keyval,
    image_output,
    image_up,
    image_up_bias,
    image_down,
    image_gains,
    image_shifts,
):
    links = Links(dp_size)
    tensor = lax.axis_index("tensor")
    pairs = text_states.shape[0] // CAP
    lens = lax.dynamic_slice_in_dim(caption_lengths, tensor * pairs, pairs, 0)
    width = text_query.shape[1]

    def packed(query, keyval):
        return jnp.concatenate([query, keyval[:, 0], keyval[:, 1]], axis=1)

    own = {
        "text_qkv": packed(text_query, text_keyval),
        "image_qkv": packed(image_query, image_keyval),
        "text_output": text_output,
        "image_output": image_output,
        "text_up": text_up,
        "image_up": image_up,
        "text_down": text_down,
        "image_down": image_down,
    }
    other = {name: links.fetch(array) for name, array in own.items()}
    bias_pair = jnp.concatenate([text_up_bias, image_up_bias])
    bias_other = links.across(bias_pair)
    text_hidden = text_up_bias.shape[0]
    parts = (own, other)

    text_qkv = [dot(text_states, part["text_qkv"]).astype(BF) for part in parts]
    image_qkv = [dot(image_states, part["image_qkv"]).astype(BF) for part in parts]
    text_ctx, image_ctx = [], []
    text_branch = image_branch = 0.0
    for k, part in enumerate(parts):
        ctx = attend_call(
            attend_kernel, lens, [text_qkv[k], image_qkv[k]], [width, width], "attend_forward"
        )
        text_ctx.append(ctx[0])
        image_ctx.append(ctx[1])
        text_branch = text_branch + dot(ctx[0], part["text_output"])
        image_branch = image_branch + dot(ctx[1], part["image_output"])

    image_out, image_dh1, image_dout, image_down_g, image_up_g, image_bias_g, image_small = (
        stream_middle(
            image_states,
            image_branch,
            image_gains.astype(F32),
            image_shifts.astype(F32),
            image_grad,
            [part["image_up"] for part in parts],
            [image_up_bias, bias_other[text_hidden:]],
            [part["image_down"] for part in parts],
        )
    )
    text_out, text_dh1, text_dout, text_down_g, text_up_g, text_bias_g, text_small = stream_middle(
        text_states,
        text_branch,
        text_gains.astype(F32),
        text_shifts.astype(F32),
        text_grad,
        [part["text_up"] for part in parts],
        [text_up_bias, bias_other[:text_hidden]],
        [part["text_down"] for part in parts],
    )
    image_down_grad = links.reduce(*image_down_g)
    image_up_grad = links.reduce(*image_up_g)
    text_down_grad = links.reduce(*text_down_g)
    text_up_grad = links.reduce(*text_up_g)

    def whole_bias(pair):
        return jnp.where(
            tensor == 0, jnp.concatenate([pair[0], pair[1]]), jnp.concatenate([pair[1], pair[0]])
        )

    small = jnp.concatenate([text_small, image_small, whole_bias(text_bias_g), whole_bias(image_bias_g)])
    small = links.reduce_small(small)
    dt, dv = text_states.shape[1], image_states.shape[1]
    text_vec = small[: 6 * dt].reshape(6, dt)
    image_vec = small[6 * dt : 6 * dt + 6 * dv].reshape(6, dv)
    rest = small[6 * dt + 6 * dv :]
    text_bias_grad = lax.dynamic_slice_in_dim(rest, tensor * text_hidden, text_hidden, 0)
    image_hidden = image_up_bias.shape[0]
    image_bias_grad = lax.dynamic_slice_in_dim(
        rest, 2 * text_hidden + tensor * image_hidden, image_hidden, 0
    )

    image_output_grad = links.reduce(*[dot_tn(ctx, image_dout).astype(BF) for ctx in image_ctx])
    text_output_grad = links.reduce(*[dot_tn(ctx, text_dout).astype(BF) for ctx in text_ctx])
    text_qkv_g, image_qkv_g = [], []
    text_in, image_in = text_dh1, image_dh1
    for k, part in enumerate(parts):
        text_dc = dot_nt(text_dout, part["text_output"]).astype(BF)
        image_dc = dot_nt(image_dout, part["image_output"]).astype(BF)
        dtext, dimage = attend_call(
            attend_back_kernel,
            lens,
            [text_qkv[k], image_qkv[k], text_dc, image_dc],
            [3 * width, 3 * width],
            "attend_backward",
        )
        text_qkv_g.append(dot_tn(text_states, dtext).astype(BF))
        image_qkv_g.append(dot_tn(image_states, dimage).astype(BF))
        text_in = text_in + dot_nt(dtext, part["text_qkv"])
        image_in = image_in + dot_nt(dimage, part["image_qkv"])
    image_qkv_grad = links.reduce(*image_qkv_g)
    text_qkv_grad = links.reduce(*text_qkv_g)

    def unpack(grad):
        return grad[:, :width], jnp.stack([grad[:, width : 2 * width], grad[:, 2 * width :]], axis=1)

    text_query_grad, text_keyval_grad = unpack(text_qkv_grad)
    image_query_grad, image_keyval_grad = unpack(image_qkv_grad)
    return (
        text_out,
        image_out,
        text_in.astype(BF),
        image_in.astype(BF),
        text_query_grad,
        text_keyval_grad,
        text_output_grad,
        text_up_grad,
        text_bias_grad,
        text_down_grad,
        text_vec[:2],
        text_vec[2:],
        image_query_grad,
        image_keyval_grad,
        image_output_grad,
        image_up_grad,
        image_bias_grad,
        image_down_grad,
        image_vec[:2],
        image_vec[2:],
    )


ROWS = P(("dp", "tensor"), None)
COLUMNS = P(None, "tensor")
KEYVAL = P(None, None, "tensor")
DOWN = P("tensor", None)
WEIGHTS = (COLUMNS, KEYVAL, DOWN, COLUMNS, P("tensor"), DOWN, P(), P())


def solution(mesh):
    return jax.shard_map(
        functools.partial(per_device, mesh.shape["dp"]),
        mesh=mesh,
        in_specs=(ROWS, ROWS, P("dp"), ROWS, ROWS) + WEIGHTS + WEIGHTS,
        out_specs=(ROWS,) * 4 + WEIGHTS + WEIGHTS,
        check_vma=False,
    )
```
